512 devices in a mesh: gx: 64 (over x, z, y_hi), gy: 8 (over y_lo, core).
Axes of the slice: x: 4, y: 8 (y_hi: 2, y_lo: 4; y = y_hi * 4 + y_lo), z: 8, core: 2. Of those that a mesh axis runs over, the one named last changes fastest.
Arguments:
- velocity: float32 [3, 128, 1024, 128], P(None, 'gx', 'gy'), may hold values from -4 to 4.5, as said below
- previous: float32 [3, 128, 1024, 128], P(None, 'gx', 'gy'), may hold values from -1800 to 1800
Outputs:
- advanced: float32 [3, 128, 1024, 128], P(None, 'gx', 'gy')
The draws below stay inside these ranges and needn't reach their ends.
Inputs may be any that keep to these rules, and one draw needn't show every extreme that they name: `velocity`: each component is zero on the two walls, the first and the last wall-normal point.
All inputs are finite; a program needn't handle non-finite values.
Results may differ from the reference program's by a relative error of at most 0.0003.
Values sent between devices are 32-bit elements; how exact they have to be, the bound alone decides.
A program may use at most 64 MiB of HBM per device.

```python
import jax
import jax.numpy as jnp
from jax import lax

NY = 1024
NZ = 128
NX = 128


def draw_velocity(key, part):
    angle = jnp.pi * jnp.arange(NY, dtype=jnp.float32) / (NY - 1)
    envelope = jnp.sin(angle) ** 2
    noise = jnp.clip(jax.random.normal(key, (3, NX, NY, NZ), jnp.float32), -4.0, 4.0)
    return noise * envelope[None, None, :, None]


def block_levels(rng, dims, pieces, least, high):
    factor_of = 1.0
    for dim, parts in pieces:
        draws = jax.random.uniform(jax.random.fold_in(jax.random.fold_in(rng, 6), dim), (parts,), jnp.float32, least / len(pieces), high / len(pieces))
        factor_of = factor_of * jnp.repeat(jnp.exp(draws), dims[dim] // parts).reshape((-1,) + (1,) * (len(dims) - 1 - dim))
    return factor_of


def bell_draw(key, extent, deviation, limit, shards=(), held_as=jnp.bfloat16):
    values = deviation * jax.random.normal(key, extent, jnp.float32)
    if shards:
        values = values * block_levels(key, extent, shards, -0.22, 0.18)
    return jnp.clip(values, -limit, limit).astype(held_as)


def setup_inputs(seed: int = 0) -> dict:
    keys = jax.random.split(jax.random.key(seed), 3)
    velocity = draw_velocity(jax.random.fold_in(keys[2], 71), 0)
    previous = bell_draw(keys[1], (3, NX, NY, NZ), 300.0, 1800.0, ((1, 64), (2, 8)), jnp.float32)
    return {"velocity": velocity, "previous": previous}


LENGTH_SPACING = 8.0 * 3.141592653589793 / 4096.0
SPAN_SPACING = 3.0 * 3.141592653589793 / 3072.0
VISCOSITY = 1.0 / 2000.0
TIME_STEP = 0.003
GAMMA_NOW = 5.0 / 12.0
ZETA_PAST = -17.0 / 60.0


def chebyshev_rows(total, offset, count):
    row_ids = offset + jnp.arange(count, dtype=jnp.int32)
    col_ids = jnp.arange(total, dtype=jnp.int32)
    row_angle = jnp.pi * row_ids.astype(jnp.float32) / (total - 1)
    col_angle = jnp.pi * col_ids.astype(jnp.float32) / (total - 1)
    on_diagonal = row_ids[:, None] == col_ids[None, :]
    parity = (row_ids[:, None] + col_ids[None, :]) % 2
    signs = 1.0 - 2.0 * parity.astype(jnp.float32)
    row_half = jnp.where((row_ids == 0) | (row_ids == total - 1), 0.5, 1.0).astype(jnp.float32)
    col_half = jnp.where((col_ids == 0) | (col_ids == total - 1), 0.5, 1.0).astype(jnp.float32)
    weight_ratio = signs * col_half[None, :] / row_half[:, None]
    spacing = -2.0 * jnp.sin(0.5 * (row_angle[:, None] + col_angle[None, :])) * jnp.sin(0.5 * (row_angle[:, None] - col_angle[None, :]))
    spacing_safe = jnp.where(on_diagonal, 1.0, spacing)
    first_off = jnp.where(on_diagonal, 0.0, weight_ratio / spacing_safe)
    first_diag = -jnp.sum(first_off, axis=1)
    first = first_off + jnp.where(on_diagonal, first_diag[:, None], 0.0)
    second_off = jnp.where(on_diagonal, 0.0, 2.0 * first_off * (first_diag[:, None] - 1.0 / spacing_safe))
    second = second_off + jnp.where(on_diagonal, -jnp.sum(second_off, axis=1)[:, None], 0.0)
    return first, second


def central(center, plus_one, minus_one, plus_two, minus_two, spacing):
    first = (8.0 * (plus_one - minus_one) - (plus_two - minus_two)) / (12.0 * spacing)
    second = (16.0 * (plus_one + minus_one) - (plus_two + minus_two) - 30.0 * center) / (12.0 * spacing * spacing)
    return first, second


def periodic(field, axis, spacing):
    return central(field, jnp.roll(field, -1, axis), jnp.roll(field, 1, axis),
                   jnp.roll(field, -2, axis), jnp.roll(field, 2, axis), spacing)


def reference(velocity, previous):
    first_matrix, second_matrix = chebyshev_rows(NY, 0, NY)
    operators = jnp.concatenate([first_matrix, second_matrix], axis=0)
    results = []
    for component in range(3):
        field = velocity[component]
        along_x, across_x = periodic(field, 0, LENGTH_SPACING)
        along_z, across_z = periodic(field, 2, SPAN_SPACING)
        stacked = jnp.einsum('ky,xyz->xkz', operators, field, precision=lax.Precision.HIGHEST)
        wall_first = stacked[:, :NY]
        wall_second = stacked[:, NY:]
        wall_term = VISCOSITY * wall_second - velocity[1] * wall_first
        plane_term = VISCOSITY * (across_x + across_z) - velocity[0] * along_x - velocity[2] * along_z
        tendency = plane_term + wall_term
        results.append(field + TIME_STEP * (GAMMA_NOW * tendency + ZETA_PAST * previous[component]))
    return jnp.stack(results)
```

```python
import functools

import jax
import jax.numpy as jnp
import numpy as np
from jax import lax
from jax.experimental import pallas as pl
from jax.experimental.pallas import tpu as pltpu
from jax.sharding import PartitionSpec as P

NY = 1024
PARTS = 8
HALVES = 2
RANKS = PARTS * HALVES
CHUNKS = 4

LENGTH_SPACING = 8.0 * 3.141592653589793 / 4096.0
SPAN_SPACING = 3.0 * 3.141592653589793 / 3072.0
VISCOSITY = 1.0 / 2000.0
TIME_STEP = 0.003
GAMMA_NOW = 5.0 / 12.0
ZETA_PAST = -17.0 / 60.0
NOW = TIME_STEP * GAMMA_NOW
MESH = pl.DeviceIdType.MESH


def chebyshev_rows(total):
    f32 = np.float32
    ids = np.arange(total)
    angle = (f32(np.pi) * ids.astype(f32)) / f32(total - 1)
    on_diagonal = np.eye(total, dtype=bool)
    signs = (1.0 - 2.0 * ((ids[:, None] + ids[None, :]) % 2)).astype(f32)
    half = np.where((ids == 0) | (ids == total - 1), 0.5, 1.0).astype(f32)
    weight_ratio = signs * half[None, :] / half[:, None]
    plus = f32(0.5) * (angle[:, None] + angle[None, :])
    minus = f32(0.5) * (angle[:, None] - angle[None, :])
    spacing = f32(-2.0) * np.sin(plus) * np.sin(minus)
    safe = np.where(on_diagonal, f32(1.0), spacing)
    off = np.where(on_diagonal, f32(0.0), weight_ratio / safe).astype(np.float64)
    diag = -off.sum(axis=1)
    first = off + np.where(on_diagonal, diag[:, None], 0.0)
    off2 = np.where(on_diagonal, 0.0, 2.0 * off * (diag[:, None] - 1.0 / safe))
    second = off2 + np.where(on_diagonal, -off2.sum(axis=1)[:, None], 0.0)
    return first, second


@functools.lru_cache(maxsize=1)
def operators():
    first, second = chebyshev_rows(NY)
    first = (first * NOW).T.reshape(CHUNKS, 256, PARTS, 128)
    second = (second * (NOW * VISCOSITY)).T.reshape(CHUNKS, 256, PARTS, 128)
    both = np.concatenate([first, second], axis=3).transpose(0, 2, 1, 3)
    high = both.astype(np.float32).astype(jnp.bfloat16)
    low = (both - high.astype(np.float64)).astype(np.float32).astype(jnp.bfloat16)
    return np.stack([high, low])


def kernel(lines, vel_hbm, prev_hbm, op_hbm, out, vel, prev, op, send, recv, below, above, acc, reply, back,
           local_sem, send_sem, recv_sem, halo_send, halo_recv, reply_sem, back_sem):
    gx, gy = lax.axis_index("gx"), lax.axis_index("gy")
    line, half = gx // 2, gx % 2
    me = half * PARTS + gy
    pair = gy // 2
    nxt, prv = lax.rem(line + 1, lines), lax.rem(line + lines - 1, lines)

    def device(rank):
        return (line * 2 + rank // PARTS, lax.rem(rank, PARTS))

    load_vel = pltpu.make_async_copy(vel_hbm, vel, local_sem.at[0])
    load_prev = pltpu.make_async_copy(prev_hbm, prev, local_sem.at[1])
    load_op = pltpu.make_async_copy(op_hbm, op, local_sem.at[2])
    load_vel.start()
    load_prev.start()
    load_op.start()

    barrier = pltpu.get_barrier_semaphore()
    for k in range(1, RANKS):
        pl.semaphore_signal(barrier, inc=1, device_id=device(lax.rem(me + k, RANKS)), device_id_type=MESH)
    for other in (nxt, prv):
        pl.semaphore_signal(barrier, inc=1, device_id=(other * 2 + half, gy), device_id_type=MESH)

    load_vel.wait()
    for c in range(3):
        for p in range(2):
            send[:, c, p] = vel[c, p].T.reshape(RANKS, 8, 128)
    pl.semaphore_wait(barrier, RANKS + 1)

    def out_copy(source, target):
        return pltpu.make_async_remote_copy(
            src_ref=send.at[target], dst_ref=recv.at[source], send_sem=send_sem.at[target],
            recv_sem=recv_sem.at[source], device_id=device(target), device_id_type=MESH)

    def others(shift):
        chip = lax.rem(pair + shift + CHUNKS, CHUNKS)
        found = []
        for h in range(HALVES):
            for core in range(2):
                if shift == 0 and h == 0 and core == 0:
                    continue
                hh = lax.rem(half + h, 2) if shift == 0 else h
                cc = lax.rem(gy + core, 2) if shift == 0 else core
                found.append(hh * PARTS + chip * 2 + cc)
        return found

    for j in (1, 3, 2, 0):
        for target in others(-j):
            out_copy(me, target).start()
    recv[me] = send[me]

    load_prev.wait()
    for p in range(2):
        w = vel[2, p]
        for c in range(3):
            f = vel[c, p]
            up, down = pltpu.roll(f, 127, 1), pltpu.roll(f, 1, 1)
            up2, down2 = pltpu.roll(f, 126, 1), pltpu.roll(f, 2, 1)
            dz = (8.0 * (up - down) - (up2 - down2)) * (NOW / (12.0 * SPAN_SPACING))
            dzz = (16.0 * (up + down) - (up2 + down2) - 30.0 * f) * (
                NOW * VISCOSITY / (12.0 * SPAN_SPACING * SPAN_SPACING))
            out[c, p] = f + dzz - w * dz + (TIME_STEP * ZETA_PAST) * prev[c, p]
    load_op.wait()

    def halo_copies(chip):
        rows = pl.ds(chip * 2, 2)
        up = pltpu.make_async_remote_copy(
            src_ref=recv.at[pl.ds(PARTS + chip * 2, 2)], dst_ref=below.at[rows], send_sem=halo_send.at[0, chip],
            recv_sem=halo_recv.at[0, chip], device_id=(nxt * 2 + half, gy), device_id_type=MESH)
        down = pltpu.make_async_remote_copy(
            src_ref=recv.at[rows], dst_ref=above.at[rows], send_sem=halo_send.at[1, chip],
            recv_sem=halo_recv.at[1, chip], device_id=(prv * 2 + half, gy), device_id_type=MESH)
        return up, down

    def products(chip):
        a = jnp.concatenate([
            jnp.concatenate([recv[h * PARTS + chip * 2 + core].reshape(48, 128) for core in range(2)], axis=1)
            for h in range(HALVES)], axis=0)
        high = a.astype(jnp.bfloat16)
        low = (a - high.astype(jnp.float32)).astype(jnp.bfloat16)
        stacked = jnp.concatenate([high, low], axis=0)

        def product(n):
            coarse = jnp.dot(stacked, op[0, chip, n], preferred_element_type=jnp.float32)
            fine = jnp.dot(high, op[1, chip, n], preferred_element_type=jnp.float32)
            return coarse[:96] + (coarse[96:] + fine)

        return product

    def reply_copy(source, target):
        return pltpu.make_async_remote_copy(
            src_ref=reply.at[target], dst_ref=back.at[source], send_sem=reply_sem.at[target],
            recv_sem=back_sem.at[source], device_id=device(target), device_id_type=MESH)

    order = (0, 1, 3, 2)
    for step, j in enumerate(order):
        chip = lax.rem(pair + j, CHUNKS)
        for source in others(j):
            out_copy(source, me).wait_recv()
        for copy in halo_copies(chip):
            copy.start()
        product = products(chip)
        if step < CHUNKS - 1:
            @pl.loop(0, PARTS)
            def _(n, product=product, step=step):
                if step == 0:
                    acc[n] = product(n)
                else:
                    acc[n] += product(n)

    def finish(n):
        walls = (acc[n] + product(n)).reshape(HALVES, 3, 2, 8, 256)
        fields = [[None] * 6 for _ in range(3)]
        for c in range(3):
            for p in range(2):
                fields[c][p] = below[n, c, p]
                fields[c][p + 2] = recv[n, c, p]
                fields[c][p + 4] = recv[PARTS + n, c, p]
            planes = fields[c] + [above[n, c, 0], above[n, c, 1]]
            fields[c] = planes
        for h in range(HALVES):
            for p in range(2):
                at = 2 + 2 * h + p
                u, v = fields[0][at], fields[1][at]
                for c in range(3):
                    f = fields[c]
                    dx = (8.0 * (f[at + 1] - f[at - 1]) - (f[at + 2] - f[at - 2])) * (
                        NOW / (12.0 * LENGTH_SPACING))
                    dxx = (16.0 * (f[at + 1] + f[at - 1]) - (f[at + 2] + f[at - 2]) - 30.0 * f[at]) * (
                        NOW * VISCOSITY / (12.0 * LENGTH_SPACING * LENGTH_SPACING))
                    first, second = walls[h, c, p, :, :128], walls[h, c, p, :, 128:]
                    reply[h * PARTS + n, c, p] = (second - v * first) + (dxx - u * dx)

    for j in (1, 3, 2, 0):
        chip = lax.rem(pair + j, CHUNKS)
        for copy in halo_copies(chip):
            copy.wait_recv()
        for core in range(2):
            finish(chip * 2 + core)
        for target in others(j):
            reply_copy(me, target).start()
    back[me] = reply[me]

    for j in (0, 1, 3, 2):
        for source in others(j):
            reply_copy(source, me).wait_recv()
    for c in range(3):
        for p in range(2):
            out[c, p] += back[:, c, p].reshape(128, 128).T

    for j in (1, 3, 2, 0):
        for target in others(j):
            out_copy(me, target).wait_send()
            reply_copy(me, target).wait_send()
        for copy in halo_copies(lax.rem(pair + j, CHUNKS)):
            copy.wait_send()


def solution(mesh):
    lines = mesh.shape["gx"] // 2

    def shards(velocity, previous):
        block = (3, 2, 128, 128)
        tiles = (RANKS, 3, 2, 8, 128)
        halo = (PARTS, 3, 2, 8, 128)
        f32 = jnp.float32
        table = operators()
        return pl.pallas_call(
            functools.partial(kernel, lines),
            out_shape=jax.ShapeDtypeStruct(block, f32),
            in_specs=[pl.BlockSpec(memory_space=pl.ANY)] * 3,
            out_specs=pl.BlockSpec(memory_space=pltpu.VMEM),
            scratch_shapes=[
                pltpu.VMEM(block, f32),
                pltpu.VMEM(block, f32),
                pltpu.VMEM(table.shape, jnp.bfloat16),
                pltpu.VMEM(tiles, f32),
                pltpu.VMEM(tiles, f32),
                pltpu.VMEM(halo, f32),
                pltpu.VMEM(halo, f32),
                pltpu.VMEM((PARTS, 96, 256), f32),
                pltpu.VMEM(tiles, f32),
                pltpu.VMEM(tiles, f32),
                pltpu.SemaphoreType.DMA((3,)),
                pltpu.SemaphoreType.DMA((RANKS,)),
                pltpu.SemaphoreType.DMA((RANKS,)),
                pltpu.SemaphoreType.DMA((2, CHUNKS)),
                pltpu.SemaphoreType.DMA((2, CHUNKS)),
                pltpu.SemaphoreType.DMA((RANKS,)),
                pltpu.SemaphoreType.DMA((RANKS,)),
            ],
            compiler_params=pltpu.CompilerParams(collective_id=0, has_side_effects=True),
        )(velocity, previous, jnp.asarray(table))

    spec = P(None, "gx", "gy", None)
    return jax.shard_map(shards, mesh=mesh, in_specs=(spec, spec), out_specs=spec, check_vma=False)
```

```python
import functools

import jax
import jax.numpy as jnp
import numpy as np
from jax import lax
from jax.experimental import pallas as pl
from jax.experimental.pallas import tpu as pltpu
from jax.sharding import PartitionSpec as P

NY = 1024
PARTS = 8
HALVES = 2
RANKS = PARTS * HALVES
CHUNKS = 4

LENGTH_SPACING = 8.0 * 3.141592653589793 / 4096.0
SPAN_SPACING = 3.0 * 3.141592653589793 / 3072.0
VISCOSITY = 1.0 / 2000.0
TIME_STEP = 0.003
GAMMA_NOW = 5.0 / 12.0
ZETA_PAST = -17.0 / 60.0
NOW = TIME_STEP * GAMMA_NOW
MESH = pl.DeviceIdType.MESH
GROUPS = ((0, 3),)
STAGES = (1, 3, 2, 0)


def chebyshev_rows(total):
    f32 = np.float32
    ids = np.arange(total)
    angle = ids.astype(f32) * (f32(np.pi) / f32(total - 1))
    on_diagonal = np.eye(total, dtype=bool)
    signs = (1.0 - 2.0 * ((ids[:, None] + ids[None, :]) % 2)).astype(f32)
    half = np.where((ids == 0) | (ids == total - 1), 0.5, 1.0).astype(f32)
    weight_ratio = signs * half[None, :] / half[:, None]
    plus = f32(0.5) * (angle[:, None] + angle[None, :])
    minus = f32(0.5) * (angle[:, None] - angle[None, :])
    spacing = f32(-2.0) * np.sin(plus) * np.sin(minus)
    safe = np.where(on_diagonal, f32(1.0), spacing)
    off = np.where(on_diagonal, f32(0.0), weight_ratio / safe).astype(np.float64)
    diag = -off.sum(axis=1)
    first = off + np.where(on_diagonal, diag[:, None], 0.0)
    off2 = np.where(on_diagonal, 0.0, 2.0 * off * (diag[:, None] - 1.0 / safe))
    second = off2 + np.where(on_diagonal, -off2.sum(axis=1)[:, None], 0.0)
    return first, second


@functools.lru_cache(maxsize=1)
def operators():
    first, second = chebyshev_rows(NY)
    first = (first * NOW).T.reshape(CHUNKS, 256, PARTS, 128)
    second = (second * (NOW * VISCOSITY)).T.reshape(CHUNKS, 256, PARTS, 128)
    both = np.concatenate([first, second], axis=3).transpose(0, 2, 1, 3)
    high = both.astype(np.float32).astype(jnp.bfloat16)
    low = (both - high.astype(np.float64)).astype(np.float32).astype(jnp.bfloat16)
    return np.stack([high, low])


def kernel(lines, vel_hbm, prev_hbm, op_hbm, out, vel, prev, op, send, recv, below, above, acc, reply, back,
           local_sem, send_sem, recv_sem, halo_send, halo_recv, reply_sem, back_sem):
    gx, gy = lax.axis_index("gx"), lax.axis_index("gy")
    line, half = gx // 2, gx % 2
    me = half * PARTS + gy
    pair = gy // 2
    nxt, prv = lax.rem(line + 1, lines), lax.rem(line + lines - 1, lines)

    def device(rank):
        return (line * 2 + rank // PARTS, lax.rem(rank, PARTS))

    load_vel = pltpu.make_async_copy(vel_hbm, vel, local_sem.at[0])
    load_prev = pltpu.make_async_copy(prev_hbm, prev, local_sem.at[1])
    load_op = pltpu.make_async_copy(op_hbm, op, local_sem.at[2])
    load_vel.start()
    load_prev.start()
    load_op.start()

    barrier = pltpu.get_barrier_semaphore()
    for k in range(1, RANKS):
        pl.semaphore_signal(barrier, inc=1, device_id=device(lax.rem(me + k, RANKS)), device_id_type=MESH)
    for other in (nxt, prv):
        pl.semaphore_signal(barrier, inc=1, device_id=(other * 2 + half, gy), device_id_type=MESH)

    load_vel.wait()
    for c in range(3):
        for p in range(2):
            send[:, c, p] = vel[c, p].T.reshape(RANKS, 8, 128)
    pl.semaphore_wait(barrier, RANKS + 1)

    def chip_at(shift):
        return lax.rem(pair + shift + CHUNKS, CHUNKS)

    def others(shift):
        found = []
        for h in range(HALVES):
            for core in range(2):
                if shift == 0 and h == 0 and core == 0:
                    continue
                hh = lax.rem(half + h, 2) if shift == 0 else h
                cc = lax.rem(gy + core, 2) if shift == 0 else core
                found.append(hh * PARTS + chip_at(shift) * 2 + cc)
        return found

    def out_copy(g, source, target):
        part = pl.ds(*GROUPS[g])
        return pltpu.make_async_remote_copy(
            src_ref=send.at[target, part], dst_ref=recv.at[source, part], send_sem=send_sem.at[g, target],
            recv_sem=recv_sem.at[g, source], device_id=device(target), device_id_type=MESH)

    def reply_copy(g, source, target):
        part = pl.ds(*GROUPS[g])
        return pltpu.make_async_remote_copy(
            src_ref=reply.at[target, part], dst_ref=back.at[source, part], send_sem=reply_sem.at[g, target],
            recv_sem=back_sem.at[g, source], device_id=device(target), device_id_type=MESH)

    def halo_copies(g, chip):
        part = pl.ds(*GROUPS[g])
        rows = pl.ds(chip * 2, 2)
        up = pltpu.make_async_remote_copy(
            src_ref=recv.at[pl.ds(PARTS + chip * 2, 2), part], dst_ref=below.at[rows, part],
            send_sem=halo_send.at[g, 0, chip], recv_sem=halo_recv.at[g, 0, chip],
            device_id=(nxt * 2 + half, gy), device_id_type=MESH)
        down = pltpu.make_async_remote_copy(
            src_ref=recv.at[rows, part], dst_ref=above.at[rows, part],
            send_sem=halo_send.at[g, 1, chip], recv_sem=halo_recv.at[g, 1, chip],
            device_id=(prv * 2 + half, gy), device_id_type=MESH)
        return up, down

    for g in range(len(GROUPS)):
        for j in STAGES:
            for target in others(-j):
                out_copy(g, me, target).start()
    recv[me] = send[me]

    load_prev.wait()
    for p in range(2):
        w = vel[2, p]
        for c in range(3):
            f = vel[c, p]
            up, down = pltpu.roll(f, 127, 1), pltpu.roll(f, 1, 1)
            up2, down2 = pltpu.roll(f, 126, 1), pltpu.roll(f, 2, 1)
            dz = (8.0 * (up - down) - (up2 - down2)) * (NOW / (12.0 * SPAN_SPACING))
            dzz = (16.0 * (up + down) - (up2 + down2) - 30.0 * f) * (
                NOW * VISCOSITY / (12.0 * SPAN_SPACING * SPAN_SPACING))
            out[c, p] = f + dzz - w * dz + (TIME_STEP * ZETA_PAST) * prev[c, p]
    load_op.wait()

    def products(g, chip):
        start, count = GROUPS[g]
        rows = 16 * count
        a = jnp.concatenate([
            jnp.concatenate([recv[h * PARTS + chip * 2 + core, start:start + count].reshape(rows, 128)
                             for core in range(2)], axis=1)
            for h in range(HALVES)], axis=0)
        high = a.astype(jnp.bfloat16)
        low = (a - high.astype(jnp.float32)).astype(jnp.bfloat16)
        stacked = jnp.concatenate([high, low], axis=0)

        def product(n):
            coarse = jnp.dot(stacked, op[0, chip, n], preferred_element_type=jnp.float32)
            fine = jnp.dot(high, op[1, chip, n], preferred_element_type=jnp.float32)
            return coarse[:2 * rows] + (coarse[2 * rows:] + fine)

        return product

    def rows_of(g):
        start, count = GROUPS[g]
        return pl.ds(32 * start, 32 * count)

    def finish(g, product, n):
        start, count = GROUPS[g]
        walls = (acc[n, rows_of(g)] + product(n)).reshape(HALVES, count, 2, 8, 256)
        columns = {}
        for c in {0, 1, *range(start, start + count)}:
            columns[c] = [below[n, c, 0], below[n, c, 1], recv[n, c, 0], recv[n, c, 1],
                          recv[PARTS + n, c, 0], recv[PARTS + n, c, 1], above[n, c, 0], above[n, c, 1]]
        for h in range(HALVES):
            for p in range(2):
                at = 2 + 2 * h + p
                u, v = columns[0][at], columns[1][at]
                for i in range(count):
                    f = columns[start + i]
                    dx = (8.0 * (f[at + 1] - f[at - 1]) - (f[at + 2] - f[at - 2])) * (
                        NOW / (12.0 * LENGTH_SPACING))
                    dxx = (16.0 * (f[at + 1] + f[at - 1]) - (f[at + 2] + f[at - 2]) - 30.0 * f[at]) * (
                        NOW * VISCOSITY / (12.0 * LENGTH_SPACING * LENGTH_SPACING))
                    first, second = walls[h, i, p, :, :128], walls[h, i, p, :, 128:]
                    reply[h * PARTS + n, start + i, p] = (second - v * first) + (dxx - u * dx)

    for g in range(len(GROUPS)):
        for step, j in enumerate(STAGES):
            chip = chip_at(j)
            for source in others(j):
                out_copy(g, source, me).wait_recv()
            for copy in halo_copies(g, chip):
                copy.start()
            product = products(g, chip)
            if step < CHUNKS - 1:
                @pl.loop(0, PARTS)
                def _(n, product=product, step=step, g=g):
                    if step == 0:
                        acc[n, rows_of(g)] = product(n)
                    else:
                        acc[n, rows_of(g)] += product(n)
        for j in STAGES:
            chip = chip_at(j)
            for copy in halo_copies(g, chip):
                copy.wait_recv()
            for core in range(2):
                finish(g, product, chip * 2 + core)
            for target in others(j):
                reply_copy(g, me, target).start()
    back[me] = reply[me]

    for g, (start, count) in enumerate(GROUPS):
        for j in STAGES:
            for source in others(j):
                reply_copy(g, source, me).wait_recv()
        for c in range(start, start + count):
            for p in range(2):
                out[c, p] += back[:, c, p].reshape(128, 128).T

    for g in range(len(GROUPS)):
        for j in STAGES:
            for target in others(j):
                out_copy(g, me, target).wait_send()
                reply_copy(g, me, target).wait_send()
            for copy in halo_copies(g, chip_at(j)):
                copy.wait_send()


def solution(mesh):
    lines = mesh.shape["gx"] // 2

    def shards(velocity, previous):
        block = (3, 2, 128, 128)
        tiles = (RANKS, 3, 2, 8, 128)
        halo = (PARTS, 3, 2, 8, 128)
        f32 = jnp.float32
        table = operators()
        groups = len(GROUPS)
        return pl.pallas_call(
            functools.partial(kernel, lines),
            out_shape=jax.ShapeDtypeStruct(block, f32),
            in_specs=[pl.BlockSpec(memory_space=pl.ANY)] * 3,
            out_specs=pl.BlockSpec(memory_space=pltpu.VMEM),
            scratch_shapes=[
                pltpu.VMEM(block, f32),
                pltpu.VMEM(block, f32),
                pltpu.VMEM(table.shape, jnp.bfloat16),
                pltpu.VMEM(tiles, f32),
                pltpu.VMEM(tiles, f32),
                pltpu.VMEM(halo, f32),
                pltpu.VMEM(halo, f32),
                pltpu.VMEM((PARTS, 96, 256), f32),
                pltpu.VMEM(tiles, f32),
                pltpu.VMEM(tiles, f32),
                pltpu.SemaphoreType.DMA((3,)),
                pltpu.SemaphoreType.DMA((groups, RANKS)),
                pltpu.SemaphoreType.DMA((groups, RANKS)),
                pltpu.SemaphoreType.DMA((groups, 2, CHUNKS)),
                pltpu.SemaphoreType.DMA((groups, 2, CHUNKS)),
                pltpu.SemaphoreType.DMA((groups, RANKS)),
                pltpu.SemaphoreType.DMA((groups, RANKS)),
            ],
            compiler_params=pltpu.CompilerParams(collective_id=0, has_side_effects=True),
        )(velocity, previous, jnp.asarray(table))

    spec = P(None, "gx", "gy", None)
    return jax.shard_map(shards, mesh=mesh, in_specs=(spec, spec), out_specs=spec, check_vma=False)
```

```python
import functools

import jax
import jax.numpy as jnp
import numpy as np
from jax import lax
from jax.experimental import pallas as pl
from jax.experimental.pallas import tpu as pltpu
from jax.sharding import PartitionSpec as P

NY = 1024
PARTS = 8
HALVES = 2
RANKS = PARTS * HALVES
DEPTH = 8
CHUNKS = 4

LENGTH_SPACING = 8.0 * 3.141592653589793 / 4096.0
SPAN_SPACING = 3.0 * 3.141592653589793 / 3072.0
VISCOSITY = 1.0 / 2000.0
TIME_STEP = 0.003
GAMMA_NOW = 5.0 / 12.0
ZETA_PAST = -17.0 / 60.0
NOW = TIME_STEP * GAMMA_NOW
MESH = pl.DeviceIdType.MESH
STAGES = (1, 3, 2, 0)


def chebyshev_rows(total):
    f32 = np.float32
    ids = np.arange(total)
    angle = ids.astype(f32) * (f32(np.pi) / f32(total - 1))
    on_diagonal = np.eye(total, dtype=bool)
    signs = (1.0 - 2.0 * ((ids[:, None] + ids[None, :]) % 2)).astype(f32)
    half = np.where((ids == 0) | (ids == total - 1), 0.5, 1.0).astype(f32)
    weight_ratio = signs * half[None, :] / half[:, None]
    plus = f32(0.5) * (angle[:, None] + angle[None, :])
    minus = f32(0.5) * (angle[:, None] - angle[None, :])
    spacing = f32(-2.0) * np.sin(plus) * np.sin(minus)
    safe = np.where(on_diagonal, f32(1.0), spacing)
    off = np.where(on_diagonal, f32(0.0), weight_ratio / safe).astype(np.float64)
    diag = -off.sum(axis=1)
    first = off + np.where(on_diagonal, diag[:, None], 0.0)
    off2 = np.where(on_diagonal, 0.0, 2.0 * off * (diag[:, None] - 1.0 / safe))
    second = off2 + np.where(on_diagonal, -off2.sum(axis=1)[:, None], 0.0)
    return first, second


@functools.lru_cache(maxsize=1)
def operators():
    first, second = chebyshev_rows(NY)
    first = (first * NOW).T.reshape(CHUNKS, 256, PARTS, 128)
    second = (second * (NOW * VISCOSITY)).T.reshape(CHUNKS, 256, PARTS, 128)
    both = np.concatenate([first, second], axis=3).transpose(0, 2, 1, 3)
    high = both.astype(np.float32).astype(jnp.bfloat16)
    low = (both - high.astype(np.float64)).astype(np.float32).astype(jnp.bfloat16)
    return np.stack([high, low])


def kernel(lines, vel_hbm, prev_hbm, op_hbm, out, vel, prev, op, send, slab, acc, reply, back,
           local_sem, send_sem, recv_sem, halo_send, halo_recv, reply_sem, back_sem, direct_sem, ready_sem):
    gx, gy = lax.axis_index("gx"), lax.axis_index("gy")
    line, half = gx // 2, gx % 2
    me = half * PARTS + gy
    pair = gy // 2
    nxt, prv = lax.rem(line + 1, lines), lax.rem(line + lines - 1, lines)
    period = min(DEPTH, lines)
    wrapped = 1 - (lax.rem(line, period) + period - 1) // period
    last = (lax.rem(line, period) + 1) // period

    def device(rank):
        return (line * 2 + rank // PARTS, lax.rem(rank, PARTS))

    load_vel = pltpu.make_async_copy(vel_hbm, vel, local_sem.at[0])
    load_prev = pltpu.make_async_copy(prev_hbm, prev, local_sem.at[1])
    load_op = pltpu.make_async_copy(op_hbm, op, local_sem.at[2])
    load_vel.start()
    load_prev.start()
    load_op.start()

    barrier = pltpu.get_barrier_semaphore()
    for k in range(1, RANKS):
        pl.semaphore_signal(barrier, inc=1, device_id=device(lax.rem(me + k, RANKS)), device_id_type=MESH)
    pl.semaphore_signal(barrier, inc=1, device_id=(prv * 2 + half, gy), device_id_type=MESH)

    @pl.when(last == 0)
    def _():
        pl.semaphore_signal(barrier, inc=1, device_id=(nxt * 2 + half, gy), device_id_type=MESH)

    @pl.when(wrapped == 1)
    def _():
        for b in range(PARTS):
            pl.semaphore_signal(barrier, inc=1, device_id=(prv * 2 + 1, b), device_id_type=MESH)

    load_vel.wait()
    for c in range(3):
        for p in range(2):
            send[:, c, p] = vel[c, p].T.reshape(RANKS, 8, 128)
    pl.semaphore_wait(barrier, RANKS + 1 - wrapped + RANKS * last * half)

    @pl.when(last == 1)
    def _():
        pl.semaphore_signal(ready_sem, inc=1, device_id=(nxt * 2 + half, gy), device_id_type=MESH)

    def chip_at(shift):
        return lax.rem(pair + shift + CHUNKS, CHUNKS)

    def others(shift):
        found = []
        for h in range(HALVES):
            for core in range(2):
                if shift == 0 and h == 0 and core == 0:
                    continue
                hh = lax.rem(half + h, 2) if shift == 0 else h
                cc = lax.rem(gy + core, 2) if shift == 0 else core
                found.append(hh * PARTS + chip_at(shift) * 2 + cc)
        return found

    def out_copy(source, target):
        return pltpu.make_async_remote_copy(
            src_ref=send.at[target], dst_ref=slab.at[1 + source // PARTS, lax.rem(source, PARTS)],
            send_sem=send_sem.at[target], recv_sem=recv_sem.at[source], device_id=device(target),
            device_id_type=MESH)

    def reply_copy(source, target):
        return pltpu.make_async_remote_copy(
            src_ref=reply.at[target], dst_ref=back.at[source], send_sem=reply_sem.at[target],
            recv_sem=back_sem.at[source], device_id=device(target), device_id_type=MESH)

    def up_copy(chip):
        rows = pl.ds(chip * 2, 2)
        return pltpu.make_async_remote_copy(
            src_ref=slab.at[2, rows], dst_ref=slab.at[0, rows], send_sem=halo_send.at[0, chip],
            recv_sem=halo_recv.at[0, chip], device_id=(nxt * 2 + half, gy), device_id_type=MESH)

    def down_copy(chip):
        rows = pl.ds(chip * 2, 2)
        return pltpu.make_async_remote_copy(
            src_ref=slab.at[1, rows], dst_ref=slab.at[3, rows], send_sem=halo_send.at[1, chip],
            recv_sem=halo_recv.at[1, chip], device_id=(prv * 2 + half, gy), device_id_type=MESH)

    def direct_copy(target):
        return pltpu.make_async_remote_copy(
            src_ref=send.at[target], dst_ref=slab.at[0, gy], send_sem=direct_sem.at[target],
            recv_sem=halo_recv.at[0, pair], device_id=(nxt * 2 + target // PARTS, lax.rem(target, PARTS)),
            device_id_type=MESH)

    def everyone(shift):
        return [h * PARTS + chip_at(shift) * 2 + core for h in range(HALVES) for core in range(2)]

    def halo_wait(h, chip):
        rows = pl.ds(chip * 2, 2)
        pltpu.make_async_remote_copy(
            src_ref=slab.at[1, rows], dst_ref=slab.at[h * 3, rows], send_sem=halo_send.at[h, chip],
            recv_sem=halo_recv.at[h, chip], device_id=(prv * 2 + half, gy), device_id_type=MESH).wait_recv()

    @pl.when(last * half == 1)
    def _():
        for j in STAGES:
            for target in everyone(-j):
                direct_copy(target).start()

    for j in STAGES:
        for target in others(-j):
            out_copy(me, target).start()
    slab[1 + half, gy] = send[me]

    load_prev.wait()
    for p in range(2):
        w = vel[2, p]
        for c in range(3):
            f = vel[c, p]
            up, down = pltpu.roll(f, 127, 1), pltpu.roll(f, 1, 1)
            up2, down2 = pltpu.roll(f, 126, 1), pltpu.roll(f, 2, 1)
            dz = (8.0 * (up - down) - (up2 - down2)) * (NOW / (12.0 * SPAN_SPACING))
            dzz = (16.0 * (up + down) - (up2 + down2) - 30.0 * f) * (
                NOW * VISCOSITY / (12.0 * SPAN_SPACING * SPAN_SPACING))
            out[c, p] = f + dzz - w * dz + (TIME_STEP * ZETA_PAST) * prev[c, p]
    load_op.wait()

    for step, j in enumerate(STAGES):
        chip = chip_at(j)
        for source in others(j):
            out_copy(source, me).wait_recv()

        @pl.when(last == 0)
        def _(chip=chip):
            up_copy(chip).start()

        @pl.when(wrapped == 0)
        def _(chip=chip):
            down_copy(chip).start()

        a = jnp.concatenate([
            jnp.concatenate([slab[1 + h, chip * 2 + core].reshape(48, 128) for core in range(2)], axis=1)
            for h in range(HALVES)], axis=0)
        high = a.astype(jnp.bfloat16)
        low = (a - high.astype(jnp.float32)).astype(jnp.bfloat16)
        stacked = jnp.concatenate([high, low], axis=0)

        @pl.loop(0, PARTS, unroll=8)
        def _(n, step=step, chip=chip, stacked=stacked, high=high):
            coarse = jnp.dot(stacked, op[0, chip, n], preferred_element_type=jnp.float32)
            fine = jnp.dot(high, op[1, chip, n], preferred_element_type=jnp.float32)
            product = (coarse[:96] + (coarse[96:] + fine)).reshape(HALVES, 48, 256)
            if step == 0:
                acc[:, n] = product
            else:
                acc[:, n] += product

    def finish(h, n):
        walls = acc[h, n].reshape(3, 2, 8, 256)
        planes = [[slab[h + q // 2, n, c, q % 2] for q in range(6)] for c in range(3)]
        for p in range(2):
            at = 2 + p
            u, v = planes[0][at], planes[1][at]
            for c in range(3):
                f = planes[c]
                dx = (8.0 * (f[at + 1] - f[at - 1]) - (f[at + 2] - f[at - 2])) * (NOW / (12.0 * LENGTH_SPACING))
                dxx = (16.0 * (f[at + 1] + f[at - 1]) - (f[at + 2] + f[at - 2]) - 30.0 * f[at]) * (
                    NOW * VISCOSITY / (12.0 * LENGTH_SPACING * LENGTH_SPACING))
                first, second = walls[c, p, :, :128], walls[c, p, :, 128:]
                reply[h * PARTS + n, c, p] = (second - v * first) + (dxx - u * dx)

    @pl.when(wrapped == 1)
    def _():
        pl.semaphore_wait(ready_sem, 1)
        for j in STAGES:
            down_copy(chip_at(j)).start()

    for j in STAGES:
        chip = chip_at(j)
        for h in range(HALVES):
            halo_wait(h, chip)
        for core in range(2):
            for h in range(HALVES):
                finish(h, chip * 2 + core)
        for target in others(j):
            reply_copy(me, target).start()
    back[me] = reply[me]

    for j in STAGES:
        for source in others(j):
            reply_copy(source, me).wait_recv()
    for c in range(3):
        for p in range(2):
            out[c, p] += back[:, c, p].reshape(128, 128).T

    for j in STAGES:
        for target in others(j):
            out_copy(me, target).wait_send()
            reply_copy(me, target).wait_send()
        down_copy(chip_at(j)).wait_send()

    @pl.when(last == 0)
    def _():
        for j in STAGES:
            up_copy(chip_at(j)).wait_send()

    @pl.when(last * half == 1)
    def _():
        for target in range(RANKS):
            direct_copy(target).wait_send()


def solution(mesh):
    lines = mesh.shape["gx"] // 2

    def shards(velocity, previous):
        block = (3, 2, 128, 128)
        tiles = (RANKS, 3, 2, 8, 128)
        f32 = jnp.float32
        table = operators()
        return pl.pallas_call(
            functools.partial(kernel, lines),
            out_shape=jax.ShapeDtypeStruct(block, f32),
            in_specs=[pl.BlockSpec(memory_space=pl.ANY)] * 3,
            out_specs=pl.BlockSpec(memory_space=pltpu.VMEM),
            scratch_shapes=[
                pltpu.VMEM(block, f32),
                pltpu.VMEM(block, f32),
                pltpu.VMEM(table.shape, jnp.bfloat16),
                pltpu.VMEM(tiles, f32),
                pltpu.VMEM((4, PARTS, 3, 2, 8, 128), f32),
                pltpu.VMEM((HALVES, PARTS, 48, 256), f32),
                pltpu.VMEM(tiles, f32),
                pltpu.VMEM(tiles, f32),
                pltpu.SemaphoreType.DMA((3,)),
                pltpu.SemaphoreType.DMA((RANKS,)),
                pltpu.SemaphoreType.DMA((RANKS,)),
                pltpu.SemaphoreType.DMA((2, CHUNKS)),
                pltpu.SemaphoreType.DMA((2, CHUNKS)),
                pltpu.SemaphoreType.DMA((RANKS,)),
                pltpu.SemaphoreType.DMA((RANKS,)),
                pltpu.SemaphoreType.DMA((RANKS,)),
                pltpu.SemaphoreType.REGULAR,
            ],
            compiler_params=pltpu.CompilerParams(collective_id=0, has_side_effects=True),
        )(velocity, previous, jnp.asarray(table))

    spec = P(None, "gx", "gy", None)
    return jax.shard_map(shards, mesh=mesh, in_specs=(spec, spec), out_specs=spec, check_vma=False)
```

```python
import functools

import jax
import jax.numpy as jnp
import numpy as np
from jax import lax
from jax.experimental import pallas as pl
from jax.experimental.pallas import tpu as pltpu
from jax.sharding import PartitionSpec as P

NY = 1024
PARTS = 8
HALVES = 2
RANKS = PARTS * HALVES
DEPTH = 8
CHUNKS = 4

LENGTH_SPACING = 8.0 * 3.141592653589793 / 4096.0
SPAN_SPACING = 3.0 * 3.141592653589793 / 3072.0
VISCOSITY = 1.0 / 2000.0
TIME_STEP = 0.003
GAMMA_NOW = 5.0 / 12.0
ZETA_PAST = -17.0 / 60.0
NOW = TIME_STEP * GAMMA_NOW
MESH = pl.DeviceIdType.MESH
STAGES = (1, 3, 2, 0)


def chebyshev_rows(total):
    f32 = np.float32
    ids = np.arange(total)
    angle = ids.astype(f32) * (f32(np.pi) / f32(total - 1))
    on_diagonal = np.eye(total, dtype=bool)
    signs = (1.0 - 2.0 * ((ids[:, None] + ids[None, :]) % 2)).astype(f32)
    half = np.where((ids == 0) | (ids == total - 1), 0.5, 1.0).astype(f32)
    weight_ratio = signs * half[None, :] / half[:, None]
    plus = f32(0.5) * (angle[:, None] + angle[None, :])
    minus = f32(0.5) * (angle[:, None] - angle[None, :])
    spacing = f32(-2.0) * np.sin(plus) * np.sin(minus)
    safe = np.where(on_diagonal, f32(1.0), spacing)
    off = np.where(on_diagonal, f32(0.0), weight_ratio / safe).astype(np.float64)
    diag = -off.sum(axis=1)
    first = off + np.where(on_diagonal, diag[:, None], 0.0)
    off2 = np.where(on_diagonal, 0.0, 2.0 * off * (diag[:, None] - 1.0 / safe))
    second = off2 + np.where(on_diagonal, -off2.sum(axis=1)[:, None], 0.0)
    return first, second


@functools.lru_cache(maxsize=1)
def operators():
    first, second = chebyshev_rows(NY)
    first = (first * NOW).T.reshape(CHUNKS, 256, PARTS, 128)
    second = (second * (NOW * VISCOSITY)).T.reshape(CHUNKS, 256, PARTS, 128)
    both = np.concatenate([first, second], axis=3).transpose(0, 2, 1, 3)
    high = both.astype(np.float32).astype(jnp.bfloat16)
    low = (both - high.astype(np.float64)).astype(np.float32).astype(jnp.bfloat16)
    return np.stack([high, low])


def kernel(lines, vel_hbm, prev_hbm, op_hbm, out, vel, prev, op, send, slab, acc, reply, back,
           local_sem, send_sem, recv_sem, halo_send, halo_recv, reply_sem, back_sem, direct_sem, ready_sem):
    gx, gy = lax.axis_index("gx"), lax.axis_index("gy")
    line, half = gx // 2, gx % 2
    me = half * PARTS + gy
    pair = gy // 2
    nxt, prv = lax.rem(line + 1, lines), lax.rem(line + lines - 1, lines)
    period = min(DEPTH, lines)
    wrapped = 1 - (lax.rem(line, period) + period - 1) // period
    last = (lax.rem(line, period) + 1) // period

    def device(rank):
        return (line * 2 + rank // PARTS, lax.rem(rank, PARTS))

    load_vel = pltpu.make_async_copy(vel_hbm, vel, local_sem.at[0])
    load_prev = pltpu.make_async_copy(prev_hbm, prev, local_sem.at[1])
    load_op = pltpu.make_async_copy(op_hbm, op, local_sem.at[2])
    load_vel.start()
    load_prev.start()
    load_op.start()

    barrier = pltpu.get_barrier_semaphore()
    for k in range(1, RANKS):
        pl.semaphore_signal(barrier, inc=1, device_id=device(lax.rem(me + k, RANKS)), device_id_type=MESH)
    pl.semaphore_signal(barrier, inc=1, device_id=(prv * 2 + half, gy), device_id_type=MESH)

    @pl.when(last == 0)
    def _():
        pl.semaphore_signal(barrier, inc=1, device_id=(nxt * 2 + half, gy), device_id_type=MESH)

    @pl.when(wrapped == 1)
    def _():
        for b in range(PARTS):
            pl.semaphore_signal(barrier, inc=1, device_id=(prv * 2 + 1, b), device_id_type=MESH)

    load_vel.wait()
    for c in range(3):
        for p in range(2):
            send[:, c, p] = vel[c, p].T.reshape(RANKS, 8, 128)
    pl.semaphore_wait(barrier, RANKS + 1 - wrapped + RANKS * last * half)

    @pl.when(last == 1)
    def _():
        pl.semaphore_signal(ready_sem, inc=1, device_id=(nxt * 2 + half, gy), device_id_type=MESH)

    def chip_at(shift):
        return lax.rem(pair + shift + CHUNKS, CHUNKS)

    def others(shift):
        found = []
        for h in range(HALVES):
            for core in range(2):
                if shift == 0 and h == 0 and core == 0:
                    continue
                hh = lax.rem(half + h, 2) if shift == 0 else h
                cc = lax.rem(gy + core, 2) if shift == 0 else core
                found.append(hh * PARTS + chip_at(shift) * 2 + cc)
        return found

    def out_copy(source, target):
        return pltpu.make_async_remote_copy(
            src_ref=send.at[target], dst_ref=slab.at[1 + source // PARTS, lax.rem(source, PARTS)],
            send_sem=send_sem.at[target], recv_sem=recv_sem.at[source], device_id=device(target),
            device_id_type=MESH)

    def reply_copy(source, target):
        return pltpu.make_async_remote_copy(
            src_ref=reply.at[target], dst_ref=back.at[source], send_sem=reply_sem.at[target],
            recv_sem=back_sem.at[source], device_id=device(target), device_id_type=MESH)

    def up_copy(chip):
        rows = pl.ds(chip * 2, 2)
        return pltpu.make_async_remote_copy(
            src_ref=slab.at[2, rows], dst_ref=slab.at[0, rows], send_sem=halo_send.at[0, chip],
            recv_sem=halo_recv.at[0, chip], device_id=(nxt * 2 + half, gy), device_id_type=MESH)

    def down_copy(chip):
        rows = pl.ds(chip * 2, 2)
        return pltpu.make_async_remote_copy(
            src_ref=slab.at[1, rows], dst_ref=slab.at[3, rows], send_sem=halo_send.at[1, chip],
            recv_sem=halo_recv.at[1, chip], device_id=(prv * 2 + half, gy), device_id_type=MESH)

    def direct_copy(target):
        return pltpu.make_async_remote_copy(
            src_ref=send.at[target], dst_ref=slab.at[0, gy], send_sem=direct_sem.at[target],
            recv_sem=halo_recv.at[0, pair], device_id=(nxt * 2 + target // PARTS, lax.rem(target, PARTS)),
            device_id_type=MESH)

    def everyone(shift):
        return [h * PARTS + chip_at(shift) * 2 + core for h in range(HALVES) for core in range(2)]

    def halo_wait(h, chip):
        rows = pl.ds(chip * 2, 2)
        pltpu.make_async_remote_copy(
            src_ref=slab.at[1, rows], dst_ref=slab.at[h * 3, rows], send_sem=halo_send.at[h, chip],
            recv_sem=halo_recv.at[h, chip], device_id=(prv * 2 + half, gy), device_id_type=MESH).wait_recv()

    @pl.when(last * half == 1)
    def _():
        for j in STAGES:
            for target in everyone(-j):
                direct_copy(target).start()

    for j in STAGES:
        for target in others(-j):
            out_copy(me, target).start()
    slab[1 + half, gy] = send[me]

    load_prev.wait()
    for p in range(2):
        w = vel[2, p]
        for c in range(3):
            f = vel[c, p]
            up, down = pltpu.roll(f, 127, 1), pltpu.roll(f, 1, 1)
            up2, down2 = pltpu.roll(f, 126, 1), pltpu.roll(f, 2, 1)
            dz = (8.0 * (up - down) - (up2 - down2)) * (NOW / (12.0 * SPAN_SPACING))
            dzz = (16.0 * (up + down) - (up2 + down2) - 30.0 * f) * (
                NOW * VISCOSITY / (12.0 * SPAN_SPACING * SPAN_SPACING))
            out[c, p] = f + dzz - w * dz + (TIME_STEP * ZETA_PAST) * prev[c, p]
    load_op.wait()

    for step, j in enumerate(STAGES):
        chip = chip_at(j)
        for source in others(j):
            out_copy(source, me).wait_recv()

        @pl.when(last == 0)
        def _(chip=chip):
            up_copy(chip).start()

        @pl.when(wrapped == 0)
        def _(chip=chip):
            down_copy(chip).start()

        a = jnp.concatenate([
            jnp.concatenate([slab[1 + h, chip * 2 + core].reshape(48, 128) for core in range(2)], axis=1)
            for h in range(HALVES)], axis=0)
        high = a.astype(jnp.bfloat16)
        low = (a - high.astype(jnp.float32)).astype(jnp.bfloat16)
        stacked = jnp.concatenate([high, low], axis=0)

        @pl.loop(0, PARTS, unroll=8)
        def _(n, step=step, chip=chip, stacked=stacked, high=high):
            coarse = jnp.dot(stacked, op[0, chip, n], preferred_element_type=jnp.float32)
            fine = jnp.dot(high, op[1, chip, n], preferred_element_type=jnp.float32)
            product = (coarse[:96] + (coarse[96:] + fine)).reshape(HALVES, 48, 256)
            if step == 0:
                acc[:, n] = product
            else:
                acc[:, n] += product

    def finish(h, n):
        walls = acc[h, n].reshape(3, 2, 8, 256)
        planes = [[slab[h + q // 2, n, c, q % 2] for q in range(6)] for c in range(3)]
        for p in range(2):
            at = 2 + p
            u, v = planes[0][at], planes[1][at]
            for c in range(3):
                f = planes[c]
                dx = (8.0 * (f[at + 1] - f[at - 1]) - (f[at + 2] - f[at - 2])) * (NOW / (12.0 * LENGTH_SPACING))
                dxx = (16.0 * (f[at + 1] + f[at - 1]) - (f[at + 2] + f[at - 2]) - 30.0 * f[at]) * (
                    NOW * VISCOSITY / (12.0 * LENGTH_SPACING * LENGTH_SPACING))
                first, second = walls[c, p, :, :128], walls[c, p, :, 128:]
                reply[h * PARTS + n, c, p] = (second - v * first) + (dxx - u * dx)

    @pl.when(wrapped == 1)
    def _():
        pl.semaphore_wait(ready_sem, 1)
        for j in STAGES:
            down_copy(chip_at(j)).start()

    for j in STAGES:
        chip = chip_at(j)
        for h in range(HALVES):
            halo_wait(h, chip)
        for core in range(2):
            for h in range(HALVES):
                finish(h, chip * 2 + core)
        for target in others(j):
            reply_copy(me, target).start()
    back[me] = reply[me]

    for j in STAGES:
        for source in others(j):
            reply_copy(source, me).wait_recv()
    for c in range(3):
        for p in range(2):
            out[c, p] += back[:, c, p].reshape(128, 128).T

    for j in STAGES:
        for target in others(j):
            out_copy(me, target).wait_send()
            reply_copy(me, target).wait_send()
        down_copy(chip_at(j)).wait_send()

    @pl.when(last == 0)
    def _():
        for j in STAGES:
            up_copy(chip_at(j)).wait_send()

    @pl.when(last * half == 1)
    def _():
        for target in range(RANKS):
            direct_copy(target).wait_send()


def solution(mesh):
    lines = mesh.shape["gx"] // 2

    def shards(velocity, previous):
        block = (3, 2, 128, 128)
        tiles = (RANKS, 3, 2, 8, 128)
        f32 = jnp.float32
        table = operators()
        return pl.pallas_call(
            functools.partial(kernel, lines),
            out_shape=jax.ShapeDtypeStruct(block, f32),
            in_specs=[pl.BlockSpec(memory_space=pl.ANY)] * 3,
            out_specs=pl.BlockSpec(memory_space=pltpu.VMEM),
            scratch_shapes=[
                pltpu.VMEM(block, f32),
                pltpu.VMEM(block, f32),
                pltpu.VMEM(table.shape, jnp.bfloat16),
                pltpu.VMEM(tiles, f32),
                pltpu.VMEM((4, PARTS, 3, 2, 8, 128), f32),
                pltpu.VMEM((HALVES, PARTS, 48, 256), f32),
                pltpu.VMEM(tiles, f32),
                pltpu.VMEM(tiles, f32),
                pltpu.SemaphoreType.DMA((3,)),
                pltpu.SemaphoreType.DMA((RANKS,)),
                pltpu.SemaphoreType.DMA((RANKS,)),
                pltpu.SemaphoreType.DMA((2, CHUNKS)),
                pltpu.SemaphoreType.DMA((2, CHUNKS)),
                pltpu.SemaphoreType.DMA((RANKS,)),
                pltpu.SemaphoreType.DMA((RANKS,)),
                pltpu.SemaphoreType.DMA((RANKS,)),
                pltpu.SemaphoreType.REGULAR,
            ],
            compiler_params=pltpu.CompilerParams(collective_id=0, has_side_effects=True, vmem_limit_bytes=24 << 20),
        )(*[pltpu.with_memory_space_constraint(x, pltpu.HBM) for x in (velocity, previous, jnp.asarray(table))])

    spec = P(None, "gx", "gy", None)
    return jax.shard_map(shards, mesh=mesh, in_specs=(spec, spec), out_specs=spec, check_vma=False)
```

```python
import functools

import jax
import jax.numpy as jnp
import numpy as np
from jax import lax
from jax.experimental import pallas as pl
from jax.experimental.pallas import tpu as pltpu
from jax.sharding import PartitionSpec as P

NY = 1024
PARTS = 8
HALVES = 2
RANKS = PARTS * HALVES
DEPTH = 8
CHUNKS = 4

LENGTH_SPACING = 8.0 * 3.141592653589793 / 4096.0
SPAN_SPACING = 3.0 * 3.141592653589793 / 3072.0
VISCOSITY = 1.0 / 2000.0
TIME_STEP = 0.003
GAMMA_NOW = 5.0 / 12.0
ZETA_PAST = -17.0 / 60.0
NOW = TIME_STEP * GAMMA_NOW
MESH = pl.DeviceIdType.MESH
STAGES = (0, 1, 3, 2)


def chebyshev_rows(total):
    f32 = np.float32
    ids = np.arange(total)
    angle = ids.astype(f32) * (f32(np.pi) / f32(total - 1))
    on_diagonal = np.eye(total, dtype=bool)
    signs = (1.0 - 2.0 * ((ids[:, None] + ids[None, :]) % 2)).astype(f32)
    half = np.where((ids == 0) | (ids == total - 1), 0.5, 1.0).astype(f32)
    weight_ratio = signs * half[None, :] / half[:, None]
    plus = f32(0.5) * (angle[:, None] + angle[None, :])
    minus = f32(0.5) * (angle[:, None] - angle[None, :])
    spacing = f32(-2.0) * np.sin(plus) * np.sin(minus)
    safe = np.where(on_diagonal, f32(1.0), spacing)
    off = np.where(on_diagonal, f32(0.0), weight_ratio / safe).astype(np.float64)
    diag = -off.sum(axis=1)
    first = off + np.where(on_diagonal, diag[:, None], 0.0)
    off2 = np.where(on_diagonal, 0.0, 2.0 * off * (diag[:, None] - 1.0 / safe))
    second = off2 + np.where(on_diagonal, -off2.sum(axis=1)[:, None], 0.0)
    return first, second


@functools.lru_cache(maxsize=1)
def operators():
    first, second = chebyshev_rows(NY)
    first = (first * NOW).T.reshape(CHUNKS, 256, PARTS, 128)
    second = (second * (NOW * VISCOSITY)).T.reshape(CHUNKS, 256, PARTS, 128)
    both = np.concatenate([first, second], axis=3).transpose(0, 2, 1, 3)
    high = both.astype(np.float32).astype(jnp.bfloat16)
    low = (both - high.astype(np.float64)).astype(np.float32).astype(jnp.bfloat16)
    return np.stack([high, low])


def kernel(lines, vel_hbm, prev_hbm, op_hbm, out, vel, prev, op, send, slab, acc, reply, back,
           local_sem, send_sem, recv_sem, halo_send, halo_recv, reply_sem, back_sem, direct_sem, ready_sem):
    gx, gy = lax.axis_index("gx"), lax.axis_index("gy")
    line, half = gx // 2, gx % 2
    me = half * PARTS + gy
    pair = gy // 2
    nxt, prv = lax.rem(line + 1, lines), lax.rem(line + lines - 1, lines)
    period = min(DEPTH, lines)
    wrapped = 1 - (lax.rem(line, period) + period - 1) // period
    last = (lax.rem(line, period) + 1) // period

    def device(rank):
        return (line * 2 + rank // PARTS, lax.rem(rank, PARTS))

    load_vel = pltpu.make_async_copy(vel_hbm, vel, local_sem.at[0])
    load_prev = pltpu.make_async_copy(prev_hbm, prev, local_sem.at[1])
    load_op = pltpu.make_async_copy(op_hbm, op, local_sem.at[2])
    load_vel.start()
    load_prev.start()
    load_op.start()

    barrier = pltpu.get_barrier_semaphore()
    for k in range(1, RANKS):
        pl.semaphore_signal(barrier, inc=1, device_id=device(lax.rem(me + k, RANKS)), device_id_type=MESH)
    pl.semaphore_signal(barrier, inc=1, device_id=(prv * 2 + half, gy), device_id_type=MESH)

    @pl.when(last == 0)
    def _():
        pl.semaphore_signal(barrier, inc=1, device_id=(nxt * 2 + half, gy), device_id_type=MESH)

    @pl.when(wrapped == 1)
    def _():
        for b in range(PARTS):
            pl.semaphore_signal(barrier, inc=1, device_id=(prv * 2 + 1, b), device_id_type=MESH)

    load_vel.wait()
    for c in range(3):
        for p in range(2):
            send[:, c, p] = vel[c, p].T.reshape(RANKS, 8, 128)
    pl.semaphore_wait(barrier, RANKS + 1 - wrapped + RANKS * last * half)

    @pl.when(last == 1)
    def _():
        pl.semaphore_signal(ready_sem, inc=1, device_id=(nxt * 2 + half, gy), device_id_type=MESH)

    def chip_at(shift):
        return lax.rem(pair + shift + CHUNKS, CHUNKS)

    def others(shift):
        found = []
        for h in range(HALVES):
            for core in range(2):
                if shift == 0 and h == 0 and core == 0:
                    continue
                hh = lax.rem(half + h, 2) if shift == 0 else h
                cc = lax.rem(gy + core, 2) if shift == 0 else core
                found.append(hh * PARTS + chip_at(shift) * 2 + cc)
        return found

    def out_copy(source, target):
        return pltpu.make_async_remote_copy(
            src_ref=send.at[target], dst_ref=slab.at[1 + source // PARTS, lax.rem(source, PARTS)],
            send_sem=send_sem.at[target], recv_sem=recv_sem.at[source], device_id=device(target),
            device_id_type=MESH)

    def reply_copy(source, target):
        return pltpu.make_async_remote_copy(
            src_ref=reply.at[target], dst_ref=back.at[source], send_sem=reply_sem.at[target],
            recv_sem=back_sem.at[source], device_id=device(target), device_id_type=MESH)

    def up_copy(chip):
        rows = pl.ds(chip * 2, 2)
        return pltpu.make_async_remote_copy(
            src_ref=slab.at[2, rows], dst_ref=slab.at[0, rows], send_sem=halo_send.at[0, chip],
            recv_sem=halo_recv.at[0, chip], device_id=(nxt * 2 + half, gy), device_id_type=MESH)

    def down_copy(chip):
        rows = pl.ds(chip * 2, 2)
        return pltpu.make_async_remote_copy(
            src_ref=slab.at[1, rows], dst_ref=slab.at[3, rows], send_sem=halo_send.at[1, chip],
            recv_sem=halo_recv.at[1, chip], device_id=(prv * 2 + half, gy), device_id_type=MESH)

    def direct_copy(target):
        return pltpu.make_async_remote_copy(
            src_ref=send.at[target], dst_ref=slab.at[0, gy], send_sem=direct_sem.at[target],
            recv_sem=halo_recv.at[0, pair], device_id=(nxt * 2 + target // PARTS, lax.rem(target, PARTS)),
            device_id_type=MESH)

    def everyone(shift):
        return [h * PARTS + chip_at(shift) * 2 + core for h in range(HALVES) for core in range(2)]

    def halo_wait(h, chip):
        rows = pl.ds(chip * 2, 2)
        pltpu.make_async_remote_copy(
            src_ref=slab.at[1, rows], dst_ref=slab.at[h * 3, rows], send_sem=halo_send.at[h, chip],
            recv_sem=halo_recv.at[h, chip], device_id=(prv * 2 + half, gy), device_id_type=MESH).wait_recv()

    @pl.when(last * half == 1)
    def _():
        for j in STAGES:
            for target in everyone(-j):
                direct_copy(target).start()

    for j in STAGES:
        for target in others(-j):
            out_copy(me, target).start()
    slab[1 + half, gy] = send[me]

    load_prev.wait()
    for p in range(2):
        w = vel[2, p]
        for c in range(3):
            f = vel[c, p]
            up, down = pltpu.roll(f, 127, 1), pltpu.roll(f, 1, 1)
            up2, down2 = pltpu.roll(f, 126, 1), pltpu.roll(f, 2, 1)
            dz = (8.0 * (up - down) - (up2 - down2)) * (NOW / (12.0 * SPAN_SPACING))
            dzz = (16.0 * (up + down) - (up2 + down2) - 30.0 * f) * (
                NOW * VISCOSITY / (12.0 * SPAN_SPACING * SPAN_SPACING))
            out[c, p] = f + dzz - w * dz + (TIME_STEP * ZETA_PAST) * prev[c, p]
    load_op.wait()

    for step, j in enumerate(STAGES):
        chip = chip_at(j)
        for source in others(j):
            out_copy(source, me).wait_recv()

        @pl.when(last == 0)
        def _(chip=chip):
            up_copy(chip).start()

        @pl.when(wrapped == 0)
        def _(chip=chip):
            down_copy(chip).start()

        a = jnp.concatenate([
            jnp.concatenate([slab[1 + h, chip * 2 + core].reshape(48, 128) for core in range(2)], axis=1)
            for h in range(HALVES)], axis=0)
        high = a.astype(jnp.bfloat16)
        low = (a - high.astype(jnp.float32)).astype(jnp.bfloat16)
        stacked = jnp.concatenate([high, low], axis=0)

        @pl.loop(0, PARTS, unroll=8)
        def _(n, step=step, chip=chip, stacked=stacked, high=high):
            coarse = jnp.dot(stacked, op[0, chip, n], preferred_element_type=jnp.float32)
            fine = jnp.dot(high, op[1, chip, n], preferred_element_type=jnp.float32)
            product = (coarse[:96] + (coarse[96:] + fine)).reshape(HALVES, 48, 256)
            if step == 0:
                acc[:, n] = product
            else:
                acc[:, n] += product

    def finish(h, n):
        walls = acc[h, n].reshape(3, 2, 8, 256)
        planes = [[slab[h + q // 2, n, c, q % 2] for q in range(6)] for c in range(3)]
        for p in range(2):
            at = 2 + p
            u, v = planes[0][at], planes[1][at]
            for c in range(3):
                f = planes[c]
                dx = (8.0 * (f[at + 1] - f[at - 1]) - (f[at + 2] - f[at - 2])) * (NOW / (12.0 * LENGTH_SPACING))
                dxx = (16.0 * (f[at + 1] + f[at - 1]) - (f[at + 2] + f[at - 2]) - 30.0 * f[at]) * (
                    NOW * VISCOSITY / (12.0 * LENGTH_SPACING * LENGTH_SPACING))
                first, second = walls[c, p, :, :128], walls[c, p, :, 128:]
                reply[h * PARTS + n, c, p] = (second - v * first) + (dxx - u * dx)

    @pl.when(wrapped == 1)
    def _():
        pl.semaphore_wait(ready_sem, 1)
        for j in STAGES:
            down_copy(chip_at(j)).start()

    for j in STAGES:
        chip = chip_at(j)
        for h in range(HALVES):
            halo_wait(h, chip)
        for core in range(2):
            for h in range(HALVES):
                finish(h, chip * 2 + core)
        for target in others(j):
            reply_copy(me, target).start()
    back[me] = reply[me]

    for j in STAGES:
        for source in others(j):
            reply_copy(source, me).wait_recv()
    for c in range(3):
        for p in range(2):
            out[c, p] += back[:, c, p].reshape(128, 128).T

    for j in STAGES:
        for target in others(j):
            out_copy(me, target).wait_send()
            reply_copy(me, target).wait_send()
        down_copy(chip_at(j)).wait_send()

    @pl.when(last == 0)
    def _():
        for j in STAGES:
            up_copy(chip_at(j)).wait_send()

    @pl.when(last * half == 1)
    def _():
        for target in range(RANKS):
            direct_copy(target).wait_send()


def solution(mesh):
    lines = mesh.shape["gx"] // 2

    def shards(velocity, previous):
        block = (3, 2, 128, 128)
        tiles = (RANKS, 3, 2, 8, 128)
        f32 = jnp.float32
        table = operators()
        return pl.pallas_call(
            functools.partial(kernel, lines),
            out_shape=jax.ShapeDtypeStruct(block, f32),
            in_specs=[pl.BlockSpec(memory_space=pl.ANY)] * 3,
            out_specs=pl.BlockSpec(memory_space=pltpu.VMEM),
            scratch_shapes=[
                pltpu.VMEM(block, f32),
                pltpu.VMEM(block, f32),
                pltpu.VMEM(table.shape, jnp.bfloat16),
                pltpu.VMEM(tiles, f32),
                pltpu.VMEM((4, PARTS, 3, 2, 8, 128), f32),
                pltpu.VMEM((HALVES, PARTS, 48, 256), f32),
                pltpu.VMEM(tiles, f32),
                pltpu.VMEM(tiles, f32),
                pltpu.SemaphoreType.DMA((3,)),
                pltpu.SemaphoreType.DMA((RANKS,)),
                pltpu.SemaphoreType.DMA((RANKS,)),
                pltpu.SemaphoreType.DMA((2, CHUNKS)),
                pltpu.SemaphoreType.DMA((2, CHUNKS)),
                pltpu.SemaphoreType.DMA((RANKS,)),
                pltpu.SemaphoreType.DMA((RANKS,)),
                pltpu.SemaphoreType.DMA((RANKS,)),
                pltpu.SemaphoreType.REGULAR,
            ],
            compiler_params=pltpu.CompilerParams(collective_id=0, has_side_effects=True, vmem_limit_bytes=24 << 20),
        )(*[pltpu.with_memory_space_constraint(x, pltpu.HBM) for x in (velocity, previous, jnp.asarray(table))])

    spec = P(None, "gx", "gy", None)
    return jax.shard_map(shards, mesh=mesh, in_specs=(spec, spec), out_specs=spec, check_vma=False)
```

```python
import functools

import jax
import jax.numpy as jnp
import numpy as np
from jax import lax
from jax.experimental import pallas as pl
from jax.experimental.pallas import tpu as pltpu
from jax.sharding import PartitionSpec as P

NY = 1024
PARTS = 8
HALVES = 2
RANKS = PARTS * HALVES
DEPTH = 8
CHUNKS = 4

LENGTH_SPACING = 8.0 * 3.141592653589793 / 4096.0
SPAN_SPACING = 3.0 * 3.141592653589793 / 3072.0
VISCOSITY = 1.0 / 2000.0
TIME_STEP = 0.003
GAMMA_NOW = 5.0 / 12.0
ZETA_PAST = -17.0 / 60.0
NOW = TIME_STEP * GAMMA_NOW
MESH = pl.DeviceIdType.MESH
STAGES = (0, 1, 3, 2)


def chebyshev_rows(total):
    f32 = np.float32
    ids = np.arange(total)
    angle = ids.astype(f32) * (f32(np.pi) / f32(total - 1))
    on_diagonal = np.eye(total, dtype=bool)
    signs = (1.0 - 2.0 * ((ids[:, None] + ids[None, :]) % 2)).astype(f32)
    half = np.where((ids == 0) | (ids == total - 1), 0.5, 1.0).astype(f32)
    weight_ratio = signs * half[None, :] / half[:, None]
    plus = f32(0.5) * (angle[:, None] + angle[None, :])
    minus = f32(0.5) * (angle[:, None] - angle[None, :])
    spacing = f32(-2.0) * np.sin(plus) * np.sin(minus)
    safe = np.where(on_diagonal, f32(1.0), spacing)
    off = np.where(on_diagonal, f32(0.0), weight_ratio / safe).astype(np.float64)
    diag = -off.sum(axis=1)
    first = off + np.where(on_diagonal, diag[:, None], 0.0)
    off2 = np.where(on_diagonal, 0.0, 2.0 * off * (diag[:, None] - 1.0 / safe))
    second = off2 + np.where(on_diagonal, -off2.sum(axis=1)[:, None], 0.0)
    return first, second


@functools.lru_cache(maxsize=1)
def operators():
    first, second = chebyshev_rows(NY)
    first = (first * NOW).T.reshape(CHUNKS, 256, PARTS, 128)
    second = (second * (NOW * VISCOSITY)).T.reshape(CHUNKS, 256, PARTS, 128)
    both = np.concatenate([first, second], axis=3).transpose(0, 2, 1, 3)
    high = both.astype(np.float32).astype(jnp.bfloat16)
    low = (both - high.astype(np.float64)).astype(np.float32).astype(jnp.bfloat16)
    return np.stack([high, low])


def kernel(lines, vel_hbm, prev_hbm, op_hbm, out, vel, prev, op, send, slab, acc, reply, back,
           local_sem, send_sem, recv_sem, halo_send, halo_recv, reply_sem, back_sem, direct_sem, ready_sem):
    gx, gy = lax.axis_index("gx"), lax.axis_index("gy")
    line, half = gx // 2, gx % 2
    me = half * PARTS + gy
    pair = gy // 2
    nxt, prv = lax.rem(line + 1, lines), lax.rem(line + lines - 1, lines)
    period = min(DEPTH, lines)
    wrapped = 1 - (lax.rem(line, period) + period - 1) // period
    last = (lax.rem(line, period) + 1) // period

    def device(rank):
        return (line * 2 + rank // PARTS, lax.rem(rank, PARTS))

    load_vel = pltpu.make_async_copy(vel_hbm, vel, local_sem.at[0])
    load_prev = pltpu.make_async_copy(prev_hbm, prev, local_sem.at[1])
    load_op = pltpu.make_async_copy(op_hbm, op, local_sem.at[2])
    load_vel.start()
    load_prev.start()
    load_op.start()

    barrier = pltpu.get_barrier_semaphore()
    pl.semaphore_signal(barrier, inc=1, device_id=(prv * 2 + half, gy), device_id_type=MESH)

    @pl.when(last == 0)
    def _():
        pl.semaphore_signal(barrier, inc=1, device_id=(nxt * 2 + half, gy), device_id_type=MESH)

    for k in range(1, RANKS):
        pl.semaphore_signal(barrier, inc=1, device_id=device(lax.rem(me + k, RANKS)), device_id_type=MESH)
    @pl.when(wrapped == 1)
    def _():
        for b in range(PARTS):
            pl.semaphore_signal(barrier, inc=1, device_id=(prv * 2 + 1, b), device_id_type=MESH)

    load_vel.wait()
    for c in range(3):
        for p in range(2):
            send[:, c, p] = vel[c, p].T.reshape(RANKS, 8, 128)
    pl.semaphore_wait(barrier, RANKS + 1 - wrapped + RANKS * last * half)

    @pl.when(last == 1)
    def _():
        pl.semaphore_signal(ready_sem, inc=1, device_id=(nxt * 2 + half, gy), device_id_type=MESH)

    def chip_at(shift):
        return lax.rem(pair + shift + CHUNKS, CHUNKS)

    def others(shift):
        found = []
        for h in range(HALVES):
            for core in range(2):
                if shift == 0 and h == 0 and core == 0:
                    continue
                hh = lax.rem(half + h, 2) if shift == 0 else h
                cc = lax.rem(gy + core, 2) if shift == 0 else core
                found.append(hh * PARTS + chip_at(shift) * 2 + cc)
        return found

    def out_copy(source, target):
        return pltpu.make_async_remote_copy(
            src_ref=send.at[target], dst_ref=slab.at[1 + source // PARTS, lax.rem(source, PARTS)],
            send_sem=send_sem.at[target], recv_sem=recv_sem.at[source], device_id=device(target),
            device_id_type=MESH)

    def reply_copy(source, target):
        return pltpu.make_async_remote_copy(
            src_ref=reply.at[target], dst_ref=back.at[source], send_sem=reply_sem.at[target],
            recv_sem=back_sem.at[source], device_id=device(target), device_id_type=MESH)

    def up_copy(chip):
        rows = pl.ds(chip * 2, 2)
        return pltpu.make_async_remote_copy(
            src_ref=slab.at[2, rows], dst_ref=slab.at[0, rows], send_sem=halo_send.at[0, chip],
            recv_sem=halo_recv.at[0, chip], device_id=(nxt * 2 + half, gy), device_id_type=MESH)

    def down_copy(chip):
        rows = pl.ds(chip * 2, 2)
        return pltpu.make_async_remote_copy(
            src_ref=slab.at[1, rows], dst_ref=slab.at[3, rows], send_sem=halo_send.at[1, chip],
            recv_sem=halo_recv.at[1, chip], device_id=(prv * 2 + half, gy), device_id_type=MESH)

    def direct_copy(target):
        return pltpu.make_async_remote_copy(
            src_ref=send.at[target], dst_ref=slab.at[0, gy], send_sem=direct_sem.at[target],
            recv_sem=halo_recv.at[0, pair], device_id=(nxt * 2 + target // PARTS, lax.rem(target, PARTS)),
            device_id_type=MESH)

    def everyone(shift):
        return [h * PARTS + chip_at(shift) * 2 + core for h in range(HALVES) for core in range(2)]

    def halo_wait(h, chip):
        rows = pl.ds(chip * 2, 2)
        pltpu.make_async_remote_copy(
            src_ref=slab.at[1, rows], dst_ref=slab.at[h * 3, rows], send_sem=halo_send.at[h, chip],
            recv_sem=halo_recv.at[h, chip], device_id=(prv * 2 + half, gy), device_id_type=MESH).wait_recv()

    @pl.when(last * half == 1)
    def _():
        for j in STAGES:
            for target in everyone(-j):
                direct_copy(target).start()

    for j in STAGES:
        for target in others(-j):
            out_copy(me, target).start()
    slab[1 + half, gy] = send[me]

    load_prev.wait()
    for p in range(2):
        w = vel[2, p]
        for c in range(3):
            f = vel[c, p]
            up, down = pltpu.roll(f, 127, 1), pltpu.roll(f, 1, 1)
            up2, down2 = pltpu.roll(f, 126, 1), pltpu.roll(f, 2, 1)
            dz = (8.0 * (up - down) - (up2 - down2)) * (NOW / (12.0 * SPAN_SPACING))
            dzz = (16.0 * (up + down) - (up2 + down2) - 30.0 * f) * (
                NOW * VISCOSITY / (12.0 * SPAN_SPACING * SPAN_SPACING))
            out[c, p] = f + dzz - w * dz + (TIME_STEP * ZETA_PAST) * prev[c, p]
    load_op.wait()

    for step, j in enumerate(STAGES):
        chip = chip_at(j)
        for source in others(j):
            out_copy(source, me).wait_recv()

        @pl.when(last == 0)
        def _(chip=chip):
            up_copy(chip).start()

        @pl.when(wrapped == 0)
        def _(chip=chip):
            down_copy(chip).start()

        a = jnp.concatenate([
            jnp.concatenate([slab[1 + h, chip * 2 + core].reshape(48, 128) for core in range(2)], axis=1)
            for h in range(HALVES)], axis=0)
        high = a.astype(jnp.bfloat16)
        low = (a - high.astype(jnp.float32)).astype(jnp.bfloat16)
        stacked = jnp.concatenate([high, low], axis=0)

        def accumulate(n, step=step, chip=chip, stacked=stacked, high=high):
            coarse = jnp.dot(stacked, op[0, chip, n], preferred_element_type=jnp.float32)
            fine = jnp.dot(high, op[1, chip, n], preferred_element_type=jnp.float32)
            product = (coarse[:96] + (coarse[96:] + fine)).reshape(HALVES, 48, 256)
            if step == 0:
                acc[:, n] = product
            else:
                acc[:, n] += product

        if step < CHUNKS - 1:
            pl.loop(0, PARTS, unroll=8)(accumulate)

    def finish(h, n):
        walls = acc[h, n].reshape(3, 2, 8, 256)
        planes = [[slab[h + q // 2, n, c, q % 2] for q in range(6)] for c in range(3)]
        for p in range(2):
            at = 2 + p
            u, v = planes[0][at], planes[1][at]
            for c in range(3):
                f = planes[c]
                dx = (8.0 * (f[at + 1] - f[at - 1]) - (f[at + 2] - f[at - 2])) * (NOW / (12.0 * LENGTH_SPACING))
                dxx = (16.0 * (f[at + 1] + f[at - 1]) - (f[at + 2] + f[at - 2]) - 30.0 * f[at]) * (
                    NOW * VISCOSITY / (12.0 * LENGTH_SPACING * LENGTH_SPACING))
                first, second = walls[c, p, :, :128], walls[c, p, :, 128:]
                reply[h * PARTS + n, c, p] = (second - v * first) + (dxx - u * dx)

    @pl.when(wrapped == 1)
    def _():
        pl.semaphore_wait(ready_sem, 1)
        for j in STAGES:
            down_copy(chip_at(j)).start()

    for j in STAGES:
        chip = chip_at(j)
        for h in range(HALVES):
            halo_wait(h, chip)
        for core in range(2):
            accumulate(chip * 2 + core)
        for core in range(2):
            for h in range(HALVES):
                finish(h, chip * 2 + core)
        for target in others(j):
            reply_copy(me, target).start()
    back[me] = reply[me]

    for j in STAGES:
        for source in others(j):
            reply_copy(source, me).wait_recv()
    for c in range(3):
        for p in range(2):
            out[c, p] += back[:, c, p].reshape(128, 128).T

    for j in STAGES:
        for target in others(j):
            out_copy(me, target).wait_send()
            reply_copy(me, target).wait_send()
        down_copy(chip_at(j)).wait_send()

    @pl.when(last == 0)
    def _():
        for j in STAGES:
            up_copy(chip_at(j)).wait_send()

    @pl.when(last * half == 1)
    def _():
        for target in range(RANKS):
            direct_copy(target).wait_send()


def solution(mesh):
    lines = mesh.shape["gx"] // 2

    def shards(velocity, previous):
        block = (3, 2, 128, 128)
        tiles = (RANKS, 3, 2, 8, 128)
        f32 = jnp.float32
        table = operators()
        return pl.pallas_call(
            functools.partial(kernel, lines),
            out_shape=jax.ShapeDtypeStruct(block, f32),
            in_specs=[pl.BlockSpec(memory_space=pl.ANY)] * 3,
            out_specs=pl.BlockSpec(memory_space=pltpu.VMEM),
            scratch_shapes=[
                pltpu.VMEM(block, f32),
                pltpu.VMEM(block, f32),
                pltpu.VMEM(table.shape, jnp.bfloat16),
                pltpu.VMEM(tiles, f32),
                pltpu.VMEM((4, PARTS, 3, 2, 8, 128), f32),
                pltpu.VMEM((HALVES, PARTS, 48, 256), f32),
                pltpu.VMEM(tiles, f32),
                pltpu.VMEM(tiles, f32),
                pltpu.SemaphoreType.DMA((3,)),
                pltpu.SemaphoreType.DMA((RANKS,)),
                pltpu.SemaphoreType.DMA((RANKS,)),
                pltpu.SemaphoreType.DMA((2, CHUNKS)),
                pltpu.SemaphoreType.DMA((2, CHUNKS)),
                pltpu.SemaphoreType.DMA((RANKS,)),
                pltpu.SemaphoreType.DMA((RANKS,)),
                pltpu.SemaphoreType.DMA((RANKS,)),
                pltpu.SemaphoreType.REGULAR,
            ],
            compiler_params=pltpu.CompilerParams(collective_id=0, has_side_effects=True, vmem_limit_bytes=24 << 20),
        )(*[pltpu.with_memory_space_constraint(x, pltpu.HBM) for x in (velocity, previous, jnp.asarray(table))])

    spec = P(None, "gx", "gy", None)
    return jax.shard_map(shards, mesh=mesh, in_specs=(spec, spec), out_specs=spec, check_vma=False)
```
